32 devices in a mesh: seq: 8 (over y, x, core), fsdp: 4 (over z).
Axes of the slice: x: 2, y: 2, z: 4, core: 2. Of those that a mesh axis runs over, the one named last changes fastest.
Arguments:
- normed: bfloat16 [32768, 1024], P(('seq', 'fsdp')), may hold values from -31 to 31, as said below
- w_qkv: bfloat16 [1024, 3072], P('fsdp'), may hold values from -0.5 to 0.5, as said below
- w_out: bfloat16 [1024, 1024], P('fsdp'), may hold values from -0.5 to 0.5
- layout: int32 [256, 10], P(('seq', 'fsdp')), may hold values from 0 to 23, as said below
- counts: int32 [256], P(('seq', 'fsdp')), may hold values from 1 to 10, as said below
Outputs:
- mixed: bfloat16 [32768, 1024], P(('seq', 'fsdp'))
The draws below stay inside these ranges and needn't reach their ends.
Inputs may be any that keep to these rules, and one draw needn't show every extreme that they name: `normed`: float activations. `w_qkv`: float weights. `layout`: each row holds 10 distinct pool entries, never the query block's own entry; entries 0 to 7 name the blocks of the station one step lower along seq, the last 8 those one step higher. `counts`: the value 10 occurs in every draw.
All inputs are finite; a program needn't handle non-finite values.
Results may differ from the reference program's by a relative error of at most 0.0099.
Values may be sent and summed in bfloat16 or wider, within the bound.
No kernel may reach another device: no remote copies, remote signals or barrier semaphores. Data moves between devices by JAX's collectives and lax.ppermute only.
A program may use at most 128 MiB of HBM per device.

```python
import math
import jax
import jax.numpy as jnp
from jax import lax

D = 1024
HEADS = 8
BLOCK = 128
KEY_BLOCKS = 10
ROWS_DEV = 1024
TOKENS = 32768
QUERY_BLOCKS = 256
N_SEQ = 8
N_FSDP = 4


def draw_normed(key, part):
    base = jax.random.truncated_normal(key, -6.0, 6.0, (TOKENS, D), jnp.float32)
    return base.astype(jnp.bfloat16)


def draw_w_qkv(key, part):
    first_key = jax.random.fold_in(jax.random.fold_in(key, 11), 0)
    base = jax.random.truncated_normal(first_key, -6.0, 6.0, (D, 3 * D), jnp.float32) / math.sqrt(D)
    query_cols = base[:, :D] * 1.7
    key_cols = base[:, D:2 * D] * 1.7
    value_cols = base[:, 2 * D:]
    joined = jnp.concatenate([query_cols, key_cols, value_cols], axis=1)
    return jnp.clip(joined, -0.5, 0.5).astype(jnp.bfloat16)


def draw_layout(key, part):
    blocks_here = ROWS_DEV // BLOCK
    pool_size = 3 * blocks_here
    raw = jax.random.randint(jax.random.fold_in(key, 23), (QUERY_BLOCKS, pool_size), 0, 1 << 20)
    column = jnp.arange(pool_size, dtype=jnp.int32)
    distinct = raw * pool_size + column[None, :]
    own_entry = blocks_here + jnp.arange(QUERY_BLOCKS, dtype=jnp.int32) % blocks_here
    distinct = jnp.where(column[None, :] == own_entry[:, None], jnp.int32(1 << 30), distinct)
    order = jnp.argsort(distinct, axis=1, stable=True)
    return order[:, :KEY_BLOCKS].astype(jnp.int32)


def draw_counts(key, part):
    drawn = jax.random.randint(jax.random.fold_in(key, 31), (QUERY_BLOCKS,), 1, KEY_BLOCKS + 1)
    first = jnp.arange(QUERY_BLOCKS, dtype=jnp.int32) == 0
    return jnp.where(first, jnp.int32(KEY_BLOCKS), drawn).astype(jnp.int32)


def levels(key, dims, cuts, least, top_value):
    gain = 1.0
    for dim, parts in cuts:
        draws = jax.random.uniform(jax.random.fold_in(jax.random.fold_in(key, 6), dim), (parts,), jnp.float32, least / len(cuts), top_value / len(cuts))
        gain = gain * jnp.repeat(jnp.exp(draws), dims[dim] // parts).reshape((-1,) + (1,) * (len(dims) - 1 - dim))
    return gain


def scatter_about(stream_key, dims, width, bound, cuts=(), held_as=jnp.bfloat16):
    array = width * jax.random.normal(stream_key, dims, jnp.float32)
    if cuts:
        array = array * levels(stream_key, dims, cuts, -0.22, 0.18)
    return jnp.clip(array, -bound, bound).astype(held_as)


def setup_inputs(seed: int = 0) -> dict:
    keys = jax.random.split(jax.random.key(seed), 6)
    return {
        "normed": draw_normed(jax.random.fold_in(keys[5], 71), 0),
        "w_qkv": draw_w_qkv(jax.random.fold_in(keys[5], 71), 0),
        "w_out": scatter_about(keys[2], (D, D), (D // 8) ** -0.5, 0.5, ((0, 4),)),
        "layout": draw_layout(jax.random.fold_in(keys[5], 71), 0),
        "counts": draw_counts(jax.random.fold_in(keys[5], 71), 0),
    }


def attend(query, own_blocks, picked, used):
    block_count = picked.shape[0]
    feature_width = query.shape[1]
    head_width = feature_width // HEADS
    keyvals = jnp.concatenate([own_blocks[:, None], picked], axis=1)
    keyvals = keyvals.reshape(block_count, (KEY_BLOCKS + 1) * BLOCK, 2 * feature_width)
    key_heads = keyvals[..., :feature_width].reshape(block_count, -1, HEADS, head_width)
    value_heads = keyvals[..., feature_width:].reshape(block_count, -1, HEADS, head_width)
    query_heads = query.reshape(block_count, BLOCK, HEADS, head_width)
    scores = jnp.einsum('bqhd,bkhd->bhqk', query_heads.astype(jnp.float32), key_heads.astype(jnp.float32))
    scores = scores * (head_width ** -0.5)
    slot_number = jnp.arange((KEY_BLOCKS + 1) * BLOCK, dtype=jnp.int32) // BLOCK
    usable = slot_number[None, :] <= used[:, None]
    scores = jnp.where(usable[:, None, None, :], scores, -jnp.inf)
    largest = jnp.max(scores, axis=-1, keepdims=True)
    expons = jnp.exp(scores - largest)
    denominator = jnp.sum(expons, axis=-1, keepdims=True)
    rounded = lax.optimization_barrier(expons.astype(jnp.bfloat16)).astype(jnp.float32)
    summed = jnp.einsum('bhqk,bkhd->bqhd', rounded, value_heads.astype(jnp.float32))
    summed = summed / jnp.transpose(denominator, (0, 2, 1, 3))
    return summed.reshape(block_count * BLOCK, feature_width).astype(jnp.bfloat16)


def reference(normed, w_qkv, w_out, layout, counts):
    stations = N_SEQ * N_FSDP
    blocks_here = ROWS_DEV // BLOCK
    shards = normed.reshape(stations, ROWS_DEV, D)
    key_weights = w_qkv[:, D:]
    query_weights = w_qkv[:, :D]

    def project_keys(shard):
        return jnp.dot(shard, key_weights, preferred_element_type=jnp.float32).astype(jnp.bfloat16)

    keyvals = lax.map(project_keys, shards)

    def one_station(station):
        span_pos = station // N_FSDP
        stream_pos = station % N_FSDP
        lower = ((span_pos - 1) % N_SEQ) * N_FSDP + stream_pos
        upper = ((span_pos + 1) % N_SEQ) * N_FSDP + stream_pos
        query = jnp.dot(shards[station], query_weights, preferred_element_type=jnp.float32).astype(jnp.bfloat16)
        pool = jnp.concatenate([keyvals[lower], keyvals[station], keyvals[upper]], axis=0)
        pool = pool.reshape(3 * blocks_here, BLOCK, 2 * D)
        first_block = (station * blocks_here).astype(jnp.int32)
        layout_here = lax.dynamic_slice_in_dim(layout, first_block, blocks_here, 0)
        counts_here = lax.dynamic_slice_in_dim(counts, first_block, blocks_here, 0)
        own_blocks = pool[blocks_here:2 * blocks_here]
        picked = pool[layout_here]
        attended = attend(query, own_blocks, picked, counts_here)
        return jnp.dot(attended, w_out, preferred_element_type=jnp.float32).astype(jnp.bfloat16)

    mixed = lax.map(one_station, jnp.arange(stations, dtype=jnp.int32))
    return mixed.reshape(TOKENS, D)
```

```python
import functools
import math

import jax
import jax.numpy as jnp
from jax import lax
from jax.experimental import pallas as pl
from jax.experimental.pallas import tpu as pltpu
from jax.sharding import PartitionSpec as P

HEADS = 8
BLOCK = 128
KEY_BLOCKS = 10
U = 4
LAG = 3


def att_kernel(slots, hw, tab, cnt, q_near, k_near, k_a, k_b, v_near, v_a, v_b, out_own, out_par,
               q_s, k_s, v_s, s_even, s_odd, m_s, l_s, acc_s, it_t, it_a, it_b, it_ok, sem):
    R, gw = k_a.shape; nh = gw//hw
    bl = R//BLOCK; T=2*bl
    cps=[]
    def go(src,dst):
        cps.append(pltpu.make_async_copy(src,dst,sem.at[len(cps)]))
    go(q_near, q_s.at[:, pl.ds(0, 2 * R)])
    go(k_near, k_s.at[pl.ds(0, 2 * R)])
    go(v_near, v_s.at[:, pl.ds(0, 2 * R)])
    for i, (k_src, v_src) in enumerate(((k_a, v_a), (k_b, v_b))):
        go(k_src, k_s.at[pl.ds((2 + i) * R, R)])
        go(v_src, v_s.at[:, pl.ds((2 + i) * R, R)])
    for cp in cps: cp.start()
    scale = hw**-0.5*math.log2(math.e)
    LEN=it_t.shape[0]
    def fill(i,c):
        it_t[i]=T; it_a[i]=0; it_b[i]=0; it_ok[i]=1
        return c
    lax.fori_loop(0,LEN,fill,0)
    def addt(t,pos):
        n=cnt[t]+1
        def addp(j,pos):
            it_t[pos]=t; it_a[pos]=tab[t*slots+2*j]
            ok=2*j+1<n
            it_b[pos]=tab[t*slots+jnp.minimum(2*j+1,slots-1)]
            it_ok[pos]=jnp.where(ok,1,0)
            return pos+1
        return lax.fori_loop(0,(n+1)//2,addp,pos)
    total=lax.fori_loop(0,T,addt,U)-U
    H=jnp.maximum((total+2*U-1)//(2*U),(LAG-1)//2)
    def init(t,c):
        m_s[t]=jnp.full(m_s.shape[1:],-jnp.inf,jnp.float32)
        l_s[t]=jnp.zeros(l_s.shape[1:],jnp.float32)
        acc_s[t]=jnp.zeros(acc_s.shape[1:],jnp.float32)
        return c
    lax.fori_loop(0,T+1,init,0)
    for cp in cps: cp.wait()
    zero=jnp.zeros((hw,BLOCK),jnp.bfloat16)
    def S(g,ref,slot):
        for u in range(U):
            i=U+g*U+u
            t=it_t[i]
            ra=pl.multiple_of(it_a[i]*BLOCK,BLOCK); rb=pl.multiple_of(it_b[i]*BLOCK,BLOCK)
            q=q_s[:, pl.ds(pl.multiple_of(t*BLOCK,BLOCK),BLOCK)]
            qbd=jnp.concatenate([jnp.concatenate([q[h*hw:(h+1)*hw] if h==hh else zero for hh in range(nh)],axis=1) for h in range(nh)],axis=0)
            k2=jnp.concatenate([k_s[pl.ds(ra,BLOCK),:],k_s[pl.ds(rb,BLOCK),:]],axis=0)
            s=jnp.dot(k2,qbd,preferred_element_type=jnp.float32)
            s0=s[:BLOCK]; s1=jnp.where(it_ok[i]>0,s[BLOCK:],-jnp.inf)
            ref[slot*U+u,:BLOCK]=s0; ref[slot*U+u,BLOCK:]=s1
            mm=jnp.max(jnp.maximum(s0,s1).reshape(BLOCK//8,8,nh*BLOCK),axis=0)
            m_s[t]=jnp.maximum(m_s[t],mm)
    def E(g,ref,slot):
        ts=[it_t[U+g*U+u] for u in range(U)]
        ms=[jnp.max(m_s[t],axis=0,keepdims=True)*scale for t in ts]
        for u in range(U):
            i=U+g*U+u
            t=ts[u]
            p=jnp.exp2(ref[slot*U+u]*scale-ms[u])
            l_s[t]=l_s[t]+jnp.sum(p.reshape(2*BLOCK//8,8,nh*BLOCK),axis=0)
            ra=pl.multiple_of(it_a[i]*BLOCK,BLOCK); rb=pl.multiple_of(it_b[i]*BLOCK,BLOCK)
            v2=jnp.concatenate([v_s[:, pl.ds(ra,BLOCK)],v_s[:, pl.ds(rb,BLOCK)]],axis=1)
            o=jnp.dot(v2,p.astype(jnp.bfloat16),preferred_element_type=jnp.float32)
            for h in range(nh):
                acc_s[t,h]=acc_s[t,h]+o[h*hw:(h+1)*hw,h*BLOCK:(h+1)*BLOCK]
    h0=(LAG-1)//2
    def pro(h,c):
        S(2*h,s_even,h&3); S(2*h+1,s_odd,h&3); return c
    def main(h,c):
        E(2*h-LAG,s_odd,(h-h0-1)&3); S(2*h,s_even,h&3)
        E(2*h-LAG+1,s_even,(h-h0)&3); S(2*h+1,s_odd,h&3)
        return c
    def epi(h,c):
        E(2*h-LAG,s_odd,(h-h0-1)&3); E(2*h-LAG+1,s_even,(h-h0)&3); return c
    lax.fori_loop(0,h0,pro,0)
    lax.fori_loop(h0,H,main,0)
    lax.fori_loop(H,H+h0+1,epi,0)
    def fin(out,t0):
        def f(t,c):
            inv=1.0/jnp.sum(l_s[t+t0],axis=0,keepdims=True)
            for h in range(nh):
                out[h*hw:(h+1)*hw,pl.ds(pl.multiple_of(t*BLOCK,BLOCK),BLOCK)]=(acc_s[t+t0,h]*inv[:,h*BLOCK:(h+1)*BLOCK]).astype(out.dtype)
            return c
        lax.fori_loop(0,bl,f,0)
    fin(out_own,0); fin(out_par,bl)


def attend(tab, cnt, q_near, k_near, k_a, k_b, v_near, v_a, v_b, hw):
    rows, gw = k_a.shape
    slots = tab.shape[0] // cnt.shape[0]
    blocks = cnt.shape[0]
    nh = gw // hw
    pairs = (slots + 1) // 2
    length = U + -(-blocks * pairs // (2 * U)) * 2 * U + 3 * U
    in_place = pl.BlockSpec(memory_space=pl.ANY)
    scalars = pl.BlockSpec(memory_space=pltpu.SMEM)
    return pl.pallas_call(
        functools.partial(att_kernel, slots, hw),
        out_shape=(jax.ShapeDtypeStruct((gw, rows), jnp.bfloat16),) * 2,
        in_specs=[scalars, scalars] + [in_place] * 7,
        out_specs=(pl.BlockSpec(memory_space=pltpu.VMEM),) * 2,
        scratch_shapes=[
            pltpu.VMEM((gw, 2 * rows + BLOCK), jnp.bfloat16),
            pltpu.VMEM((4 * rows, gw), jnp.bfloat16),
            pltpu.VMEM((gw, 4 * rows), jnp.bfloat16),
            pltpu.VMEM((4 * U, 2 * BLOCK, nh * BLOCK), jnp.float32),
            pltpu.VMEM((4 * U, 2 * BLOCK, nh * BLOCK), jnp.float32),
            pltpu.VMEM((blocks + 1, 8, nh * BLOCK), jnp.float32),
            pltpu.VMEM((blocks + 1, 8, nh * BLOCK), jnp.float32),
            pltpu.VMEM((blocks + 1, nh, hw, BLOCK), jnp.float32),
            pltpu.SMEM((length,), jnp.int32),
            pltpu.SMEM((length,), jnp.int32),
            pltpu.SMEM((length,), jnp.int32),
            pltpu.SMEM((length,), jnp.int32),
            pltpu.SemaphoreType.DMA((7,)),
        ],
        compiler_params=pltpu.CompilerParams(vmem_limit_bytes=48 * 2**20),
        cost_estimate=pl.CostEstimate(
            flops=8 * rows * slots * BLOCK * gw,
            bytes_accessed=14 * rows * gw * 2,
            transcendentals=2 * rows * slots * BLOCK * nh,
        ),
    )(tab, cnt, q_near, k_near, k_a, k_b, v_near, v_a, v_b)


def column_major(w, x):
    return lax.dot_general(
        w, x, (((0,), (1,)), ((), ())), preferred_element_type=jnp.float32
    ).astype(jnp.bfloat16)


def row_major(x, w):
    return jnp.dot(x, w, preferred_element_type=jnp.float32).astype(jnp.bfloat16)


def shards(normed, w_qkv, w_out, layout, counts):
    rows, width = normed.shape
    blocks = rows // BLOCK
    n_seq = lax.axis_size("seq")
    n_fsdp = lax.axis_size("fsdp")
    assert n_seq % 8 == 0
    place = lax.axis_index("seq")
    level = lax.axis_index("fsdp")
    core = place % 2
    side = (place // 4) % 2
    groups = 4
    gw = width // groups
    hw = width // HEADS
    shard = w_qkv.shape[0]

    def swap(value, bit):
        return lax.ppermute(value, "seq", [(i, i ^ bit) for i in range(n_seq)])

    def from_level(value, steps):
        return lax.ppermute(
            value, "fsdp", [(i, (i - steps) % n_fsdp) for i in range(n_fsdp)]
        )

    far_a = lax.ppermute(
        normed, "seq", [(i, (i + 1) % n_seq if i % 2 else (i - 1) % n_seq) for i in range(n_seq)]
    )
    mine = 2 * core + side
    other = 2 * core + 1 - side

    def columns(group):
        w = w_qkv.reshape(shard, 3, groups, gw)
        return lax.dynamic_index_in_dim(w, group, 2, keepdims=False).reshape(shard, 3 * gw)

    w_mine = columns(mine)
    z_mine = [from_level(w_mine, k) for k in range(1, n_fsdp)]
    partner = swap(normed, 1)
    table = jnp.concatenate([counts[:, None], layout], axis=1)
    tables = jnp.concatenate([table, swap(table, 1)], axis=0)
    z_other = [swap(piece, 4) for piece in z_mine]
    far_b = swap(far_a, 1)

    out_piece = lax.dynamic_slice_in_dim(w_out, mine * gw, gw, 1)
    out_rows = jnp.zeros((n_fsdp * shard, gw), w_out.dtype)
    for k in range(n_fsdp):
        piece = out_piece if k == 0 else from_level(out_piece, k)
        out_rows = lax.dynamic_update_slice_in_dim(
            out_rows, piece, ((level + k) % n_fsdp) * shard, 0
        )
    out_both = jnp.concatenate([out_rows, swap(out_rows, 4)], axis=0)
    out_partner = swap(out_both, 1)

    count = tables[:, 0]
    entry = tables[:, 1:]
    is_partner = (jnp.arange(2 * blocks, dtype=jnp.int32) >= blocks).astype(jnp.int32)[:, None]
    chain = entry // blocks + (core + is_partner * (1 - 2 * core))
    even = jnp.where(chain == 0, 2, jnp.where(chain == 3, 3, chain - 1))
    odd = jnp.where(chain == 0, 3, jnp.where(chain == 3, 2, 2 - chain))
    stored = jnp.where(core == 0, even, odd) * blocks + entry % blocks
    own = jnp.arange(2 * blocks, dtype=jnp.int32)[:, None]
    key_table = jnp.concatenate([own, stored], axis=1).reshape(-1)

    near = jnp.concatenate([normed, partner], axis=0)

    def group_part(own_piece, pieces):
        parts = []
        for part in range(3):
            w = jnp.zeros((n_fsdp * shard, gw), w_qkv.dtype)
            for k, piece in enumerate([own_piece] + pieces):
                w = lax.dynamic_update_slice_in_dim(
                    w, piece[:, part * gw : (part + 1) * gw], ((level + k) % n_fsdp) * shard, 0
                )
            parts.append(w)
        w_q, w_k, w_v = parts
        return attend(
            key_table,
            count,
            column_major(w_q, near),
            row_major(near, w_k),
            row_major(far_a, w_k),
            row_major(far_b, w_k),
            column_major(w_v, near),
            column_major(w_v, far_a),
            column_major(w_v, far_b),
            hw,
        )

    attended = jnp.zeros((width, rows), jnp.bfloat16)
    for group, theirs, own_piece, pieces in (
        (mine, 2 * (1 - core) + side, w_mine, z_mine),
        (other, 2 * (1 - core) + 1 - side, columns(other), z_other),
    ):
        att_own, att_partner = group_part(own_piece, pieces)
        attended = lax.dynamic_update_slice_in_dim(attended, att_own, group * gw, 0)
        attended = lax.dynamic_update_slice_in_dim(attended, swap(att_partner, 1), theirs * gw, 0)

    full_out = jnp.zeros((n_fsdp * shard, width), w_out.dtype)
    depth = n_fsdp * shard
    for source, first, second in (
        (out_both, mine, other),
        (out_partner, 2 * (1 - core) + side, 2 * (1 - core) + 1 - side),
    ):
        full_out = lax.dynamic_update_slice_in_dim(full_out, source[:depth], first * gw, 1)
        full_out = lax.dynamic_update_slice_in_dim(full_out, source[depth:], second * gw, 1)
    return lax.dot_general(
        attended, full_out, (((0,), (0,)), ((), ())), preferred_element_type=jnp.float32
    ).astype(jnp.bfloat16)


def solution(mesh):
    return jax.shard_map(
        shards,
        mesh=mesh,
        in_specs=(
            P(("seq", "fsdp"), None),
            P("fsdp", None),
            P("fsdp", None),
            P(("seq", "fsdp"), None),
            P(("seq", "fsdp")),
        ),
        out_specs=P(("seq", "fsdp"), None),
        check_vma=False,
    )
```

```python
import functools
import math

import jax
import jax.numpy as jnp
from jax import lax
from jax.experimental import pallas as pl
from jax.experimental.pallas import tpu as pltpu
from jax.sharding import PartitionSpec as P

HEADS = 8
BLOCK = 128
KEY_BLOCKS = 10
U = 4
LAG = 3


def plan_kernel(near_len, far_len, core_ref, own, partner, near, far, made):
    blocks, slots = own.shape
    empty = 2 * blocks + (1 << 24)
    core = core_ref[0]

    def clear(i, carry):
        near[i] = empty
        far[i] = empty
        return carry

    def clear_rest(i, carry):
        near[i] = empty
        return carry

    lax.fori_loop(0, far_len, clear, 0)
    lax.fori_loop(far_len, near_len, clear_rest, 0)

    def station(source, which, start):
        def block(b, starts):
            t = which * blocks + b
            made[0] = 0
            made[1] = 0
            near[starts[0]] = t + t * 256 + t * 65536

            def slot(j, carry):
                entry = source[b, j]
                link = lax.div(entry, blocks) + jnp.where(core == which, 0, 1)
                rest = lax.rem(entry, blocks)
                is_near = jnp.logical_and(link > 0, link < 3)

                def put(out, kind, first, position):
                    item = first + lax.shift_right_logical(made[kind], 1)
                    odd = made[kind] & 1
                    fresh = t + position * 256 + position * 65536
                    paired = (out[item] & 65535) + position * 65536 + (1 << 24)
                    out[item] = jnp.where(odd == 1, paired, fresh)
                    made[kind] = made[kind] + 1

                @pl.when(is_near)
                def _():
                    put(near, 0, starts[0], jnp.where(link - 1 == core, 0, blocks) + rest)

                @pl.when(jnp.logical_not(is_near))
                def _():
                    mine = jnp.where(core == 0, link == 0, link == 3)
                    put(far, 1, starts[1], jnp.where(mine, 0, blocks) + rest)

                return carry

            made[0] = 1
            lax.fori_loop(1, source[b, 0] + 1, slot, 0)
            return (
                starts[0] + lax.shift_right_logical(made[0] + 1, 1),
                starts[1] + lax.shift_right_logical(made[1] + 1, 1),
            )

        return lax.fori_loop(0, blocks, block, start)

    ends = station(partner, 1, station(own, 0, (U, U)))
    near[near_len - 1] = ends[0] - U
    far[far_len - 1] = ends[1] - U


def list_length(blocks, most):
    return U + -(-blocks * ((most + 1) // 2) // (2 * U)) * 2 * U + 3 * U + 1


def make_plan(core, own, partner):
    blocks, slots = own.shape
    near_len = list_length(2 * blocks, slots)
    far_len = list_length(2 * blocks, min(slots - 1, blocks))
    smem = pl.BlockSpec(memory_space=pltpu.SMEM)
    return pl.pallas_call(
        functools.partial(plan_kernel, near_len, far_len),
        out_shape=(
            jax.ShapeDtypeStruct((near_len,), jnp.int32),
            jax.ShapeDtypeStruct((far_len,), jnp.int32),
        ),
        in_specs=[smem] * 3,
        out_specs=(smem, smem),
        scratch_shapes=[pltpu.SMEM((2,), jnp.int32)],
        name="plan",
    )(core, own, partner)


def load_weights(pieces, level, w_s, row_from, sems):
    shard = pieces[0].shape[1]
    copies = []
    for k, piece in enumerate(pieces):
        column = pl.multiple_of(lax.rem(level + k, len(pieces)) * shard, shard)
        copies.append(
            pltpu.make_async_copy(
                piece.at[pl.ds(row_from, w_s.shape[0])], w_s.at[:, pl.ds(column, shard)], sems.at[k]
            )
        )
    return copies


def run_items(items, last, hw, q_s, k_s, v_s, s_even, s_odd, m_s, l_s, acc_s):
    gw = k_s.shape[1]
    nh = gw // hw
    scale = hw**-0.5 * math.log2(math.e)
    total = items[last]
    steps = jnp.maximum((total + 2 * U - 1) // (2 * U), (LAG - 1) // 2)
    zero = jnp.zeros((hw, BLOCK), jnp.bfloat16)

    def fields(i):
        word = items[i]
        t = word & 255
        a = (word >> 8) & 255
        b = (word >> 16) & 255
        return (
            t,
            pl.multiple_of(a * BLOCK, BLOCK),
            pl.multiple_of(b * BLOCK, BLOCK),
            word >> 24,
        )

    def scores(g, ref, slot):
        for u in range(U):
            t, ra, rb, both = fields(U + g * U + u)
            q = q_s[:, pl.ds(pl.multiple_of(t * BLOCK, BLOCK), BLOCK)]
            diagonal = jnp.concatenate(
                [
                    jnp.concatenate(
                        [q[h * hw : (h + 1) * hw] if h == other else zero for other in range(nh)],
                        axis=1,
                    )
                    for h in range(nh)
                ],
                axis=0,
            )
            keys = jnp.concatenate([k_s[pl.ds(ra, BLOCK), :], k_s[pl.ds(rb, BLOCK), :]], axis=0)
            s = jnp.dot(keys, diagonal, preferred_element_type=jnp.float32)
            s0 = s[:BLOCK]
            s1 = jnp.where(both > 0, s[BLOCK:], -jnp.inf)
            ref[slot * U + u, :BLOCK] = s0
            ref[slot * U + u, BLOCK:] = s1
            top = jnp.max(jnp.maximum(s0, s1).reshape(BLOCK // 8, 8, nh * BLOCK), axis=0)
            m_s[t] = jnp.maximum(m_s[t], top)

    def sums(g, ref, slot):
        parts = [fields(U + g * U + u) for u in range(U)]
        tops = [jnp.max(m_s[part[0]], axis=0, keepdims=True) * scale for part in parts]
        for u in range(U):
            t, ra, rb, _ = parts[u]
            p = jnp.exp2(ref[slot * U + u] * scale - tops[u])
            l_s[t] = l_s[t] + jnp.sum(p.reshape(2 * BLOCK // 8, 8, nh * BLOCK), axis=0)
            values = jnp.concatenate([v_s[:, pl.ds(ra, BLOCK)], v_s[:, pl.ds(rb, BLOCK)]], axis=1)
            o = jnp.dot(values, p.astype(jnp.bfloat16), preferred_element_type=jnp.float32)
            for h in range(nh):
                acc_s[t, h] = acc_s[t, h] + o[h * hw : (h + 1) * hw, h * BLOCK : (h + 1) * BLOCK]

    first = (LAG - 1) // 2

    def start(h, carry):
        scores(2 * h, s_even, h & 3)
        scores(2 * h + 1, s_odd, h & 3)
        return carry

    def main(h, carry):
        sums(2 * h - LAG, s_odd, (h - first - 1) & 3)
        scores(2 * h, s_even, h & 3)
        sums(2 * h - LAG + 1, s_even, (h - first) & 3)
        scores(2 * h + 1, s_odd, h & 3)
        return carry

    def finish(h, carry):
        sums(2 * h - LAG, s_odd, (h - first - 1) & 3)
        sums(2 * h - LAG + 1, s_even, (h - first) & 3)
        return carry

    lax.fori_loop(0, first, start, 0)
    lax.fori_loop(first, steps, main, 0)
    lax.fori_loop(steps, steps + first + 1, finish, 0)


def transposed(a, b):
    return lax.dot_general(a, b, (((1,), (1,)), ((), ())), preferred_element_type=jnp.float32)


def near_kernel(
    hw, n_pieces, level_ref, items, x_own, x_partner, *rest
):
    pieces = rest[:n_pieces]
    q_out, m_out, l_out, acc_out, x_s, w_s, q_s, k_s, v_s, s_even, s_odd, w_sem, x_sem, o_sem = rest[
        n_pieces:
    ]
    rows = x_own.shape[0]
    gw = k_s.shape[1]
    chunk = x_s.shape[0] // x_sem.shape[0]
    per = rows // chunk
    w_copies = load_weights(pieces, level_ref[0], w_s, 0, w_sem)
    for copy in w_copies:
        copy.start()
    x_copies = []
    for i, source in enumerate((x_own, x_partner)):
        for j in range(per):
            x_copies.append(
                pltpu.make_async_copy(
                    source.at[pl.ds(j * chunk, chunk)],
                    x_s.at[pl.ds(i * rows + j * chunk, chunk)],
                    x_sem.at[i * per + j],
                )
            )
            x_copies[-1].start()
    blocks = m_out.shape[0] - 1

    def clear(t, carry):
        m_out[t] = jnp.full(m_out.shape[1:], -jnp.inf, jnp.float32)
        l_out[t] = jnp.zeros(l_out.shape[1:], jnp.float32)
        acc_out[t] = jnp.zeros(acc_out.shape[1:], jnp.float32)
        return carry

    lax.fori_loop(0, blocks + 1, clear, 0)
    for copy in w_copies:
        copy.wait()

    def project(i, carry):
        here = pl.multiple_of(i * chunk, chunk)
        pltpu.make_async_copy(
            x_own.at[pl.ds(0, chunk)], x_s.at[pl.ds(here, chunk)], x_sem.at[i]
        ).wait()
        x = x_s[pl.ds(here, chunk), :]
        k_s[pl.ds(here, chunk), :] = transposed(x, w_s[2 * gw :, :]).astype(jnp.bfloat16)
        q_s[:, pl.ds(here, chunk)] = transposed(w_s[:gw, :], x).astype(jnp.bfloat16)
        v_s[:, pl.ds(here, chunk)] = transposed(w_s[gw : 2 * gw, :], x).astype(jnp.bfloat16)
        return carry

    lax.fori_loop(0, 2 * per, project, 0)
    out_copy = pltpu.make_async_copy(q_s.at[:, pl.ds(0, 2 * rows)], q_out, o_sem)
    out_copy.start()
    run_items(items, items.shape[0] - 1, hw, q_s, k_s, v_s, s_even, s_odd, m_out, l_out, acc_out)
    out_copy.wait()


def far_kernel(hw, n_pieces, level_ref, items, x_a, x_b, q_in, m_in, l_in, acc_in, *rest):
    pieces = rest[:n_pieces]
    (
        out_own,
        out_partner,
        x_s,
        w_s,
        q_s,
        k_s,
        v_s,
        s_even,
        s_odd,
        m_s,
        l_s,
        acc_s,
        w_sem,
        x_sem,
        o_sem,
    ) = rest[n_pieces:]
    rows = x_a.shape[0]
    gw = k_s.shape[1]
    nh = gw // hw
    chunk = x_s.shape[0] // x_sem.shape[0]
    per = rows // chunk
    w_copies = load_weights(pieces, level_ref[0], w_s, gw, w_sem)
    for copy in w_copies:
        copy.start()
    for i, source in enumerate((x_a, x_b)):
        for j in range(per):
            pltpu.make_async_copy(
                source.at[pl.ds(j * chunk, chunk)],
                x_s.at[pl.ds(i * rows + j * chunk, chunk)],
                x_sem.at[i * per + j],
            ).start()
    q_copy = pltpu.make_async_copy(q_in, q_s.at[:, pl.ds(0, 2 * rows)], o_sem)
    q_copy.start()
    blocks = m_in.shape[0] - 1

    def clear(t, carry):
        m_s[t] = m_in[t]
        l_s[t] = jnp.zeros(l_s.shape[1:], jnp.float32)
        acc_s[t] = jnp.zeros(acc_s.shape[1:], jnp.float32)
        return carry

    lax.fori_loop(0, blocks + 1, clear, 0)
    for copy in w_copies:
        copy.wait()

    def project(i, carry):
        here = pl.multiple_of(i * chunk, chunk)
        pltpu.make_async_copy(
            x_a.at[pl.ds(0, chunk)], x_s.at[pl.ds(here, chunk)], x_sem.at[i]
        ).wait()
        x = x_s[pl.ds(here, chunk), :]
        k_s[pl.ds(here, chunk), :] = transposed(x, w_s[gw:, :]).astype(jnp.bfloat16)
        v_s[:, pl.ds(here, chunk)] = transposed(w_s[:gw, :], x).astype(jnp.bfloat16)
        return carry

    lax.fori_loop(0, 2 * per, project, 0)
    q_copy.wait()
    run_items(items, items.shape[0] - 1, hw, q_s, k_s, v_s, s_even, s_odd, m_s, l_s, acc_s)
    scale = hw**-0.5 * math.log2(math.e)

    def put(out, offset):
        def one(b, carry):
            t = offset + b
            before = jnp.max(m_in[t], axis=0, keepdims=True)
            top = jnp.max(m_s[t], axis=0, keepdims=True)
            fade = jnp.exp2((before - top) * scale)
            total = fade * jnp.sum(l_in[t], axis=0, keepdims=True)
            total = total + jnp.sum(l_s[t], axis=0, keepdims=True)
            inverse = 1.0 / total
            for h in range(nh):
                lanes = slice(h * BLOCK, (h + 1) * BLOCK)
                value = acc_in[t, h] * fade[:, lanes] + acc_s[t, h]
                out[h * hw : (h + 1) * hw, pl.ds(pl.multiple_of(b * BLOCK, BLOCK), BLOCK)] = (
                    value * inverse[:, lanes]
                ).astype(out.dtype)
            return carry

        lax.fori_loop(0, blocks // 2, one, 0)

    put(out_own, 0)
    put(out_partner, blocks // 2)


def specs():
    return (
        pl.BlockSpec(memory_space=pltpu.SMEM),
        pl.BlockSpec(memory_space=pl.ANY),
        pl.BlockSpec(memory_space=pltpu.VMEM),
    )


def loop_scratch(rows, gw, hw):
    nh = gw // hw
    return [
        pltpu.VMEM((gw, 2 * rows + BLOCK), jnp.bfloat16),
        pltpu.VMEM((2 * rows, gw), jnp.bfloat16),
        pltpu.VMEM((gw, 2 * rows), jnp.bfloat16),
        pltpu.VMEM((4 * U, 2 * BLOCK, nh * BLOCK), jnp.float32),
        pltpu.VMEM((4 * U, 2 * BLOCK, nh * BLOCK), jnp.float32),
    ]


def near_part(level, items, x_own, x_partner, pieces, hw):
    rows, width = x_own.shape
    gw = pieces[0].shape[0] // 3
    nh = gw // hw
    blocks = 2 * rows // BLOCK
    smem, anywhere, vmem = specs()
    state = (
        jax.ShapeDtypeStruct((blocks + 1, 8, nh * BLOCK), jnp.float32),
        jax.ShapeDtypeStruct((blocks + 1, 8, nh * BLOCK), jnp.float32),
        jax.ShapeDtypeStruct((blocks + 1, nh, hw, BLOCK), jnp.float32),
    )
    chunks = max(2, 2 * rows // 512)
    return pl.pallas_call(
        functools.partial(near_kernel, hw, len(pieces)),
        out_shape=(jax.ShapeDtypeStruct((gw, 2 * rows), jnp.bfloat16),) + state,
        in_specs=[smem, smem] + [anywhere] * (2 + len(pieces)),
        out_specs=(anywhere, vmem, vmem, vmem),
        scratch_shapes=[
            pltpu.VMEM((2 * rows, width), jnp.bfloat16),
            pltpu.VMEM((3 * gw, width), jnp.bfloat16),
        ]
        + loop_scratch(rows, gw, hw)
        + [
            pltpu.SemaphoreType.DMA((len(pieces),)),
            pltpu.SemaphoreType.DMA((chunks,)),
            pltpu.SemaphoreType.DMA,
        ],
        compiler_params=pltpu.CompilerParams(vmem_limit_bytes=48 * 2**20),
        cost_estimate=pl.CostEstimate(
            flops=16 * rows * width * gw, bytes_accessed=30 * 2**20, transcendentals=0
        ),
        name="near",
    )(level, items, x_own, x_partner, *pieces)


def far_part(level, items, x_a, x_b, pieces, q, m, l, acc, hw):
    rows, width = x_a.shape
    gw = q.shape[0]
    smem, anywhere, vmem = specs()
    chunks = max(2, 2 * rows // 512)
    return pl.pallas_call(
        functools.partial(far_kernel, hw, len(pieces)),
        out_shape=(jax.ShapeDtypeStruct((gw, rows), jnp.bfloat16),) * 2,
        in_specs=[smem, smem] + [anywhere] * 3 + [vmem] * 3 + [anywhere] * len(pieces),
        out_specs=(vmem, vmem),
        scratch_shapes=[
            pltpu.VMEM((2 * rows, width), jnp.bfloat16),
            pltpu.VMEM((2 * gw, width), jnp.bfloat16),
        ]
        + loop_scratch(rows, gw, hw)
        + [
            pltpu.VMEM(m.shape, jnp.float32),
            pltpu.VMEM(l.shape, jnp.float32),
            pltpu.VMEM(acc.shape, jnp.float32),
            pltpu.SemaphoreType.DMA((len(pieces),)),
            pltpu.SemaphoreType.DMA((chunks,)),
            pltpu.SemaphoreType.DMA,
        ],
        compiler_params=pltpu.CompilerParams(vmem_limit_bytes=48 * 2**20),
        cost_estimate=pl.CostEstimate(
            flops=10 * rows * width * gw, bytes_accessed=20 * 2**20, transcendentals=0
        ),
        name="far",
    )(level, items, x_a, x_b, q, m, l, acc, *pieces)


def shards(normed, w_qkv, w_out, layout, counts):
    rows, width = normed.shape
    n_seq = lax.axis_size("seq")
    n_fsdp = lax.axis_size("fsdp")
    assert n_seq % 8 == 0
    place = lax.axis_index("seq")
    level = lax.axis_index("fsdp")
    core = place % 2
    side = (place // 4) % 2
    groups = 4
    gw = width // groups
    hw = width // HEADS
    shard = w_qkv.shape[0]

    def swap(value, bit):
        return lax.ppermute(value, "seq", [(i, i ^ bit) for i in range(n_seq)])

    def from_level(value, steps):
        return lax.ppermute(
            value, "fsdp", [(i, (i - steps) % n_fsdp) for i in range(n_fsdp)]
        )

    mine = 2 * core + side
    other = 2 * core + 1 - side
    theirs = 2 * (1 - core) + side
    theirs_other = 2 * (1 - core) + 1 - side

    def columns(group):
        parts = []
        for part in (0, 2, 1):
            w = lax.dynamic_slice_in_dim(w_qkv, part * width + group * gw, gw, 1)
            parts.append(w.T)
        return jnp.concatenate(parts, axis=0)

    w_mine = columns(mine)
    z_mine = [from_level(w_mine, k) for k in range(1, n_fsdp)]
    far_a = lax.ppermute(
        normed, "seq", [(i, (i + 1) % n_seq if i % 2 else (i - 1) % n_seq) for i in range(n_seq)]
    )
    partner = swap(normed, 1)
    table = jnp.concatenate([counts[:, None], layout], axis=1)
    near_items, far_items = make_plan(core[None], table, swap(table, 1))
    z_other = [swap(piece, 4) for piece in z_mine]
    far_b = swap(far_a, 1)

    out_piece = lax.dynamic_slice_in_dim(w_out, mine * gw, gw, 1)
    out_rows = jnp.zeros((n_fsdp * shard, gw), w_out.dtype)
    for k in range(n_fsdp):
        piece = out_piece if k == 0 else from_level(out_piece, k)
        out_rows = lax.dynamic_update_slice_in_dim(
            out_rows, piece, ((level + k) % n_fsdp) * shard, 0
        )
    out_both = jnp.concatenate([out_rows, swap(out_rows, 4)], axis=0)
    out_partner = swap(out_both, 1)

    attended = jnp.zeros((width, rows), jnp.bfloat16)
    for group, sender, pieces in (
        (mine, theirs, [w_mine] + z_mine),
        (other, theirs_other, [columns(other)] + z_other),
    ):
        q, m, l, acc = near_part(level[None], near_items, normed, partner, pieces, hw)
        att_own, att_partner = far_part(
            level[None], far_items, far_a, far_b, pieces, q, m, l, acc, hw
        )
        attended = lax.dynamic_update_slice_in_dim(attended, att_own, group * gw, 0)
        attended = lax.dynamic_update_slice_in_dim(attended, swap(att_partner, 1), sender * gw, 0)

    depth = n_fsdp * shard
    full_out = jnp.zeros((depth, width), w_out.dtype)
    for source, first, second in (
        (out_both, mine, other),
        (out_partner, theirs, theirs_other),
    ):
        full_out = lax.dynamic_update_slice_in_dim(full_out, source[:depth], first * gw, 1)
        full_out = lax.dynamic_update_slice_in_dim(full_out, source[depth:], second * gw, 1)
    return lax.dot_general(
        attended, full_out, (((0,), (0,)), ((), ())), preferred_element_type=jnp.float32
    ).astype(jnp.bfloat16)


def solution(mesh):
    return jax.shard_map(
        shards,
        mesh=mesh,
        in_specs=(
            P(("seq", "fsdp"), None),
            P("fsdp", None),
            P("fsdp", None),
            P(("seq", "fsdp"), None),
            P(("seq", "fsdp")),
        ),
        out_specs=P(("seq", "fsdp"), None),
        check_vma=False,
    )
```
